32 devices in a mesh: dp: 16 (over z, y, core), tensor: 2 (over x).
Axes of the slice: x: 2, y: 2, z: 4, core: 2. Of those that a mesh axis runs over, the one named last changes fastest.
Arguments:
- latents: bfloat16 [16384, 1024], P(('dp', 'tensor')), may hold values from -6 to 6
- inputs: bfloat16 [65536, 1024], P(('dp', 'tensor')), may hold values from -6 to 6
- frames: int32 [128], replicated, may hold values from 4 to 16, as said below
- group_clip: int32 [128], P('dp'), may hold values from 0 to 127, each once
- norm_gain: float32 [4, 1024], replicated, may hold values from 0.5 to 1.5
- norm_bias: float32 [4, 1024], replicated, may hold values from -2 to 2
- cross_q: bfloat16 [1024, 1024], P(None, 'tensor'), may hold values from -0.1875 to 0.1875
- cross_k: bfloat16 [1024, 1024], P(None, 'tensor'), may hold values from -0.1875 to 0.1875
- cross_v: bfloat16 [1024, 1024], P(None, 'tensor'), may hold values from -0.1875 to 0.1875
- cross_o: bfloat16 [1024, 1024], P('tensor'), may hold values from -1 to 1
- self_q: bfloat16 [1024, 1024], P(None, 'tensor'), may hold values from -0.1875 to 0.1875
- self_k: bfloat16 [1024, 1024], P(None, 'tensor'), may hold values from -0.1875 to 0.1875
- self_v: bfloat16 [1024, 1024], P(None, 'tensor'), may hold values from -0.1875 to 0.1875
- self_o: bfloat16 [1024, 1024], P('tensor'), may hold values from -0.75 to 0.75
- mlp_up: bfloat16 [1024, 4096], P(None, 'tensor'), may hold values from -0.1875 to 0.1875
- up_bias: bfloat16 [4096], P('tensor'), may hold values from -3 to 3
- mlp_down: bfloat16 [4096, 1024], P('tensor'), may hold values from -0.09375 to 0.09375
- out_bias: float32 [3, 1024], replicated, may hold values from -2 to 2
- cotangent: bfloat16 [16384, 1024], P(('dp', 'tensor')), may hold values from -6 to 6
Outputs:
- result: bfloat16 [16384, 1024], P(('dp', 'tensor'))
- d_latents: float32 [16384, 1024], P(('dp', 'tensor'))
- d_inputs: float32 [65536, 1024], P(('dp', 'tensor'))
- d_norm_gain: float32 [4, 1024], replicated
- d_norm_bias: float32 [4, 1024], replicated
- d_out_bias: float32 [3, 1024], replicated
- d_cross_q: float32 [1024, 1024], P(None, 'tensor')
- d_cross_k: float32 [1024, 1024], P(None, 'tensor')
- d_cross_v: float32 [1024, 1024], P(None, 'tensor')
- d_cross_o: float32 [1024, 1024], P('tensor')
- d_self_q: float32 [1024, 1024], P(None, 'tensor')
- d_self_k: float32 [1024, 1024], P(None, 'tensor')
- d_self_v: float32 [1024, 1024], P(None, 'tensor')
- d_self_o: float32 [1024, 1024], P('tensor')
- d_mlp_up: float32 [1024, 4096], P(None, 'tensor')
- d_up_bias: float32 [4096], P('tensor')
- d_mlp_down: float32 [4096, 1024], P('tensor')
The draws below stay inside these ranges and needn't reach their ends.
Inputs may be any that keep to these rules, and one draw needn't show every extreme that they name: Each clip has 4 or 16 frames, and both counts occur. `group_clip`: every clip index belongs to exactly one group.
All inputs are finite; a program needn't handle non-finite values.
Results may differ from the reference program's by a relative error of at most 0.03.
Values may be sent and summed in bfloat16 or wider, within the bound.
A program may use at most 256 MiB of HBM per device.

```python
import jax
import jax.numpy as jnp
from jax import lax

D = 1024
HEADS = 8
HS = 128
FF = 4096
LAT = 128
FRAME_SLOTS = 16
FRAME_ROWS = 32
SHORT_FRAMES = 4
IN_ROWS = 512
G = 128
NL = 16384
NI = 65536


def draw_frames(key, part):
    chooser = jax.random.randint(key, (G,), 0, 2)
    counts = SHORT_FRAMES + (FRAME_SLOTS - SHORT_FRAMES) * chooser
    counts = counts.at[0].set(SHORT_FRAMES).at[1].set(FRAME_SLOTS)
    return counts.astype(jnp.int32)


def steps_of(key, extent, cuts, least, largest):
    level, own = 1.0, jax.random.fold_in(key, 6)
    for axis_at, shards_of in cuts:
        draws = jnp.exp(jax.random.uniform(jax.random.fold_in(own, axis_at), (shards_of,), jnp.float32, least / len(cuts), largest / len(cuts)))
        level = level * jnp.repeat(draws, extent[axis_at] // shards_of).reshape([-1 if axis == axis_at else 1 for axis in range(len(extent))])
    return level


def noise(key, shape, deviation, limit, shards=(), kind=jnp.bfloat16):
    array = jax.random.normal(key, shape, jnp.float32) * deviation
    if len(shards) > 0:
        array = steps_of(key, shape, shards, -0.22, 0.18) * array
    return jnp.clip(array, min=-limit, max=limit).astype(kind)


def setup_inputs(seed: int = 0) -> dict:
    arg_keys = jax.random.split(jax.random.key(seed), 20)
    latents = noise(arg_keys[0], (NL, D), 1.0, 6.0, ((0, 32),))
    inputs = noise(arg_keys[1], (NI, D), 1.0, 6.0, ((0, 32),))
    frames = draw_frames(jax.random.fold_in(arg_keys[19], 71), 0)
    group_clip = jax.random.permutation(arg_keys[3], G).astype(jnp.int32)
    norm_gain = jnp.clip(1.0 + 0.1 * jax.random.normal(arg_keys[4], (4, D), jnp.float32), 0.5, 1.5)
    norm_bias = noise(arg_keys[5], (4, D), 0.3, 2.0, (), jnp.float32)
    cross_q = noise(arg_keys[6], (D, D), D ** -0.5, 0.1875, ((1, 2),))
    cross_k = noise(arg_keys[7], (D, D), D ** -0.5, 0.1875, ((1, 2),))
    cross_v = noise(arg_keys[8], (D, D), D ** -0.5, 0.1875, ((1, 2),))
    cross_o = noise(arg_keys[9], (D, D), (D // 32) ** -0.5, 1.0, ((0, 2),))
    self_q = noise(arg_keys[10], (D, D), D ** -0.5, 0.1875, ((1, 2),))
    self_k = noise(arg_keys[11], (D, D), D ** -0.5, 0.1875, ((1, 2),))
    self_v = noise(arg_keys[12], (D, D), D ** -0.5, 0.1875, ((1, 2),))
    self_o = noise(arg_keys[13], (D, D), (D // 16) ** -0.5, 0.75, ((0, 2),))
    mlp_up = noise(arg_keys[14], (D, FF), D ** -0.5, 0.1875, ((1, 2),))
    up_bias = noise(arg_keys[15], (FF,), 0.5, 3.0, ((0, 2),))
    mlp_down = noise(arg_keys[16], (FF, D), FF ** -0.5, 0.09375, ((0, 2),))
    out_bias = noise(arg_keys[17], (3, D), 0.3, 2.0, (), jnp.float32)
    cotangent = noise(arg_keys[18], (NL, D), 1.0, 6.0, ((0, 32),))
    return {"latents": latents, "inputs": inputs, "frames": frames, "group_clip": group_clip, "norm_gain": norm_gain, "norm_bias": norm_bias, "cross_q": cross_q, "cross_k": cross_k, "cross_v": cross_v, "cross_o": cross_o, "self_q": self_q, "self_k": self_k, "self_v": self_v, "self_o": self_o, "mlp_up": mlp_up, "up_bias": up_bias, "mlp_down": mlp_down, "out_bias": out_bias, "cotangent": cotangent}


@jax.custom_vjp
def low(v):
    return lax.optimization_barrier(v.astype(jnp.bfloat16)).astype(jnp.float32)

@jax.custom_vjp
def low_back(v):
    return v

def low_keep(v):
    return (low(v), None)

def low_pass(kept, grad):
    return (grad,)

def back_keep(v):
    return (v, None)

def back_low(kept, grad):
    return (low(grad),)
low.defvjp(low_keep, low_pass)
low_back.defvjp(back_keep, back_low)
HIGHEST = lax.Precision.HIGHEST
EPSILON = 1e-05
NEG_LARGE = -1e+30
GELU_COEF = 0.7978845608028654
GELU_CUBE = 0.044715

def matmul(left, right):
    return jnp.dot(left, right, precision=HIGHEST, preferred_element_type=jnp.float32)

def layer_norm(values, gain, shift):
    average = lax.optimization_barrier(jnp.mean(values, axis=-1, keepdims=True))
    centered = values - average
    variance = lax.optimization_barrier(jnp.mean(centered * centered, axis=-1, keepdims=True))
    return centered * lax.rsqrt(variance + EPSILON) * gain + shift

def gelu_tanh(values):
    inner = GELU_COEF * (values + GELU_CUBE * values * values * values)
    return 0.5 * values * (1.0 + jnp.tanh(inner))

def attend(queries, key_vecs, value_vecs, lengths):
    groups = lengths.shape[0]
    key_count = key_vecs.shape[0] // groups
    query_heads = queries.reshape(groups, LAT, HEADS, HS)
    key_heads = key_vecs.reshape(groups, key_count, HEADS, HS)
    value_heads = value_vecs.reshape(groups, key_count, HEADS, HS)
    scores = jnp.einsum('gqhd,gkhd->ghqk', query_heads, key_heads, precision=HIGHEST) * HS ** (-0.5)
    visible = jnp.arange(key_count, dtype=jnp.int32)[None, None, None, :] < lengths[:, None, None, None]
    scores = low_back(jnp.where(visible, scores, NEG_LARGE))
    row_max = lax.optimization_barrier(jnp.max(scores, axis=-1, keepdims=True))
    exponent = jnp.exp(scores - row_max)
    probability = exponent / lax.optimization_barrier(jnp.sum(exponent, axis=-1, keepdims=True))
    mixed = jnp.einsum('ghqk,gkhd->gqhd', low(probability), value_heads, precision=HIGHEST)
    return low(low_back(mixed.reshape(groups * LAT, HEADS * HS)))

def block_layer(params, lat_block, in_block, lengths):
    norm_gain, norm_bias, cross_q, cross_k, cross_v, cross_o, self_q, self_k, self_v, self_o, mlp_up, up_bias, mlp_down, out_bias = params
    groups = lengths.shape[0]
    normed = low(layer_norm(lat_block, norm_gain[0], norm_bias[0]))
    in_normed = low(layer_norm(in_block, norm_gain[1], norm_bias[1]))
    mixed = attend(low(low_back(matmul(normed, cross_q))), low(low_back(matmul(in_normed, cross_k))), low(low_back(matmul(in_normed, cross_v))), lengths)
    stream = lat_block + low_back(matmul(mixed, cross_o)) + out_bias[0]
    normed = low(layer_norm(stream, norm_gain[2], norm_bias[2]))
    full_lengths = jnp.full((groups,), LAT, jnp.int32)
    mixed = attend(low(low_back(matmul(normed, self_q))), low(low_back(matmul(normed, self_k))), low(low_back(matmul(normed, self_v))), full_lengths)
    stream = stream + low_back(matmul(mixed, self_o)) + out_bias[1]
    normed = low(layer_norm(stream, norm_gain[3], norm_bias[3]))
    pre = low_back(matmul(normed, mlp_up) + up_bias)
    hidden = low(gelu_tanh(pre))
    return stream + low_back(matmul(hidden, mlp_down)) + out_bias[2]

def forward(params, latents32, inputs32, lengths):
    block_count = lengths.shape[0] // 4
    lat_blocks = latents32.reshape(block_count, 4 * LAT, D)
    in_blocks = inputs32.reshape(block_count, 4 * IN_ROWS, D)
    len_blocks = lengths.reshape(block_count, 4)
    checked = jax.checkpoint(block_layer)

    def scan_step(carry, pieces):
        lat_block, in_block, len_block = pieces
        return (carry, checked(params, lat_block, in_block, len_block))
    carry_end, outputs = lax.scan(scan_step, jnp.zeros((), jnp.float32), (lat_blocks, in_blocks, len_blocks))
    return outputs.reshape(NL, D)

def reference(latents, inputs, frames, group_clip, norm_gain, norm_bias, cross_q, cross_k, cross_v, cross_o, self_q, self_k, self_v, self_o, mlp_up, up_bias, mlp_down, out_bias, cotangent):
    lengths = (frames[group_clip] * FRAME_ROWS).astype(jnp.int32)
    params = tuple((argument.astype(jnp.float32) for argument in (norm_gain, norm_bias, cross_q, cross_k, cross_v, cross_o, self_q, self_k, self_v, self_o, mlp_up, up_bias, mlp_down, out_bias)))

    def whole_layer(param_set, lat32, in32):
        return forward(param_set, lat32, in32, lengths)
    output, pullback = jax.vjp(whole_layer, params, latents.astype(jnp.float32), inputs.astype(jnp.float32))
    param_grads, d_latents, d_inputs = pullback(cotangent.astype(jnp.float32))
    g_gain, g_shift, g_cross_q, g_cross_k, g_cross_v, g_cross_o, g_self_q, g_self_k, g_self_v, g_self_o, g_up, g_up_bias, g_down, g_out_bias = param_grads
    return (output.astype(jnp.bfloat16), d_latents, d_inputs, g_gain, g_shift, g_out_bias, g_cross_q, g_cross_k, g_cross_v, g_cross_o, g_self_q, g_self_k, g_self_v, g_self_o, g_up, g_up_bias, g_down)
```

```python
from types import SimpleNamespace

import jax
import jax.numpy as jnp
from jax import lax
from jax.experimental import pallas as pl
from jax.experimental.pallas import tpu as pltpu
from jax.sharding import PartitionSpec as P

AXES = ("dp", "tensor")
HS = 128
LAT = 128
FRAME_ROWS = 32


EPSILON = 1e-05
NEG_LARGE = -1e30
GELU_COEF = 0.7978845608028654
GELU_CUBE = 0.044715


def layer_norm(values, gain, shift):
    average = jnp.mean(values, axis=-1, keepdims=True)
    centered = values - average
    variance = jnp.mean(centered * centered, axis=-1, keepdims=True)
    return centered * lax.rsqrt(variance + EPSILON) * gain + shift


def gelu_tanh(values):
    inner = GELU_COEF * (values + GELU_CUBE * values * values * values)
    return 0.5 * values * (1.0 + jnp.tanh(inner))


def gelu_slope(values):
    squared = values * values
    hyperbolic = jnp.tanh(GELU_COEF * (values + GELU_CUBE * squared * values))
    return 0.5 * (1.0 + hyperbolic) + 0.5 * values * (1.0 - hyperbolic * hyperbolic) * GELU_COEF * (
        1.0 + 3.0 * GELU_CUBE * squared
    )


def matmul(left, right):
    return jnp.dot(left, right, preferred_element_type=jnp.float32)


def gram_left(left, right):
    return lax.dot_general(
        left, right, (((0,), (0,)), ((), ())), preferred_element_type=jnp.float32
    )


def times_transposed(left, right):
    return lax.dot_general(
        left, right, (((1,), (1,)), ((), ())), preferred_element_type=jnp.float32
    )


def block_size(groups):
    chosen = 1
    for candidate in (4, 3, 2):
        if chosen == 1 and groups % candidate == 0:
            chosen = candidate
    return chosen


def split_blocks(array, groups, head_size):
    block = block_size(groups)
    rows = array.shape[0] // groups
    heads = array.shape[1] // head_size
    return array.reshape(groups // block, block, rows, heads, head_size)


def masked_scores(query_block, key_block, length_block, head_size):
    key_count = key_block.shape[1]
    scores = jnp.einsum(
        "gqhd,gkhd->ghqk", query_block, key_block, preferred_element_type=jnp.float32
    ) * head_size ** (-0.5)
    positions = lax.broadcasted_iota(jnp.int32, (1, 1, 1, key_count), 3)
    return jnp.where(positions < length_block[:, None, None, None], scores, NEG_LARGE)


def attend_forward(queries, key_vecs, value_vecs, lengths, head_size):
    groups = lengths.shape[0]
    block = block_size(groups)
    pieces = (
        split_blocks(queries, groups, head_size),
        split_blocks(key_vecs, groups, head_size),
        split_blocks(value_vecs, groups, head_size),
        lengths.reshape(groups // block, block),
    )

    def one_block(piece):
        query_block, key_block, value_block, length_block = piece
        scores = masked_scores(query_block, key_block, length_block, head_size)
        row_max = jnp.max(scores, axis=-1, keepdims=True)
        exponent = jnp.exp(scores - row_max)
        row_total = jnp.sum(exponent, axis=-1, keepdims=True)
        probability = (exponent / row_total).astype(jnp.bfloat16)
        mixed = jnp.einsum(
            "ghqk,gkhd->gqhd", probability, value_block, preferred_element_type=jnp.float32
        )
        return (mixed.astype(jnp.bfloat16), (row_max + jnp.log(row_total))[..., 0])

    mixed, log_total = lax.map(one_block, pieces)
    return (mixed.reshape(queries.shape), log_total)


def attend_backward(queries, key_vecs, value_vecs, grad_mixed, log_total, lengths, head_size):
    groups = lengths.shape[0]
    block = block_size(groups)
    pieces = (
        split_blocks(queries, groups, head_size),
        split_blocks(key_vecs, groups, head_size),
        split_blocks(value_vecs, groups, head_size),
        split_blocks(grad_mixed, groups, head_size),
        log_total,
        lengths.reshape(groups // block, block),
    )
    scale_factor = head_size ** (-0.5)

    def one_block(piece):
        query_block, key_block, value_block, grad_block, total_block, length_block = piece
        scores = masked_scores(query_block, key_block, length_block, head_size)
        probability = jnp.exp(scores - total_block[..., None])
        grad_prob = jnp.einsum(
            "gqhd,gkhd->ghqk", grad_block, value_block, preferred_element_type=jnp.float32
        )
        inner = jnp.sum(probability * grad_prob, axis=-1, keepdims=True)
        grad_score = (probability * (grad_prob - inner)).astype(jnp.bfloat16)
        grad_query = (
            jnp.einsum("ghqk,gkhd->gqhd", grad_score, key_block, preferred_element_type=jnp.float32)
            * scale_factor
        )
        grad_key = (
            jnp.einsum(
                "ghqk,gqhd->gkhd", grad_score, query_block, preferred_element_type=jnp.float32
            )
            * scale_factor
        )
        grad_value = jnp.einsum(
            "ghqk,gqhd->gkhd",
            probability.astype(jnp.bfloat16),
            grad_block,
            preferred_element_type=jnp.float32,
        )
        return (
            grad_query.astype(jnp.bfloat16),
            grad_key.astype(jnp.bfloat16),
            grad_value.astype(jnp.bfloat16),
        )

    grad_query, grad_key, grad_value = lax.map(one_block, pieces)
    return (
        grad_query.reshape(queries.shape),
        grad_key.reshape(key_vecs.shape),
        grad_value.reshape(value_vecs.shape),
    )


def gather_rows(normed):
    return lax.all_gather(normed, AXES[1], axis=0, tiled=True)


def gather_grads(grads):
    return lax.all_gather(grads, AXES[1], axis=0, tiled=True)


def branch_sum(mixed, weight, own_rows):

    def term(begin_row, row_count):
        return matmul(mixed, weight)

    return lax.psum_scatter(
        term(jnp.int32(0), lax.axis_size(AXES[1]) * own_rows),
        AXES[1],
        scatter_dimension=0,
        tiled=True,
    )


def back_rows(term, own_rows):
    return lax.psum_scatter(
        term(jnp.int32(0), own_rows * lax.axis_size(AXES[1])).astype(jnp.bfloat16),
        AXES[1],
        scatter_dimension=0,
        tiled=True,
    ).astype(jnp.float32)


def back_inputs(term, own_rows):
    return lax.psum_scatter(
        term(jnp.int32(0), own_rows * lax.axis_size(AXES[1])).astype(jnp.bfloat16),
        AXES[1],
        scatter_dimension=0,
        tiled=True,
    ).astype(jnp.float32)


def split_shards(
    latents,
    inputs,
    frames,
    group_clip,
    norm_gain,
    norm_bias,
    cross_q,
    cross_k,
    cross_v,
    cross_o,
    self_q,
    self_k,
    self_v,
    self_o,
    mlp_up,
    up_bias,
    mlp_down,
    out_bias,
    cotangent,
):
    head_size = HS
    own_rows = latents.shape[0]
    own_inputs = inputs.shape[0]
    stream = latents.astype(jnp.float32)
    source = inputs.astype(jnp.float32)
    lat_normed = layer_norm(stream, norm_gain[0], norm_bias[0]).astype(jnp.bfloat16)
    in_normed = layer_norm(source, norm_gain[1], norm_bias[1]).astype(jnp.bfloat16)
    local_set = (
        cross_q,
        cross_k,
        cross_v,
        cross_o,
        self_q,
        self_k,
        self_v,
        self_o,
        mlp_up,
        up_bias,
        mlp_down,
    )
    rows_cross, rows_input = (
        lax.all_gather(lat_normed, AXES[1], axis=0, tiled=True),
        lax.all_gather(in_normed, AXES[1], axis=0, tiled=True),
    )
    (
        w_cross_q,
        w_cross_k,
        w_cross_v,
        w_cross_o,
        w_self_q,
        w_self_k,
        w_self_v,
        w_self_o,
        w_up,
        b_up,
        w_down,
    ) = local_set
    matches = group_clip[:, None] == lax.broadcasted_iota(jnp.int32, (1, frames.shape[0]), 1)
    lengths = jnp.sum(jnp.where(matches, frames[None, :], 0), axis=1) * FRAME_ROWS
    full_lengths = jnp.full(lengths.shape, LAT, jnp.int32)
    cross_query = matmul(rows_cross, w_cross_q).astype(jnp.bfloat16)
    cross_keys = matmul(rows_input, w_cross_k).astype(jnp.bfloat16)
    cross_values = matmul(rows_input, w_cross_v).astype(jnp.bfloat16)
    cross_mixed, cross_total = attend_forward(
        cross_query, cross_keys, cross_values, lengths, head_size
    )
    stream1 = stream + branch_sum(cross_mixed, w_cross_o, own_rows) + out_bias[0]
    self_normed = layer_norm(stream1, norm_gain[2], norm_bias[2]).astype(jnp.bfloat16)
    rows_self = gather_rows(self_normed)
    self_query = matmul(rows_self, w_self_q).astype(jnp.bfloat16)
    self_keys = matmul(rows_self, w_self_k).astype(jnp.bfloat16)
    self_values = matmul(rows_self, w_self_v).astype(jnp.bfloat16)
    self_mixed, self_total = attend_forward(
        self_query, self_keys, self_values, full_lengths, head_size
    )
    stream2 = stream1 + branch_sum(self_mixed, w_self_o, own_rows) + out_bias[1]
    mlp_normed = layer_norm(stream2, norm_gain[3], norm_bias[3]).astype(jnp.bfloat16)
    rows_mlp = gather_rows(mlp_normed)
    pre_act = matmul(rows_mlp, w_up) + b_up.astype(jnp.float32)
    hidden = gelu_tanh(pre_act).astype(jnp.bfloat16)
    stream3 = stream2 + branch_sum(hidden, w_down, own_rows) + out_bias[2]
    result = stream3.astype(jnp.bfloat16)
    grad3 = cotangent.astype(jnp.float32)
    rows_grad3 = gather_grads(grad3.astype(jnp.bfloat16))
    d_down = gram_left(hidden, rows_grad3)
    d_pre = (times_transposed(rows_grad3, w_down) * gelu_slope(pre_act)).astype(jnp.bfloat16)
    d_upb = jnp.sum(d_pre.astype(jnp.float32), axis=0)
    d_up = gram_left(rows_mlp, d_pre)
    d_mlp_rows = back_rows(lambda begin_row, row_count: times_transposed(d_pre, w_up), own_rows)
    ln_value, ln_pull = jax.vjp(layer_norm, stream2, norm_gain[3], norm_bias[3])
    d_stream2, gain_three, shift_three = ln_pull(d_mlp_rows)
    grad2 = grad3 + d_stream2
    rows_grad2 = gather_grads(grad2.astype(jnp.bfloat16))
    self_query = matmul(rows_self, w_self_q).astype(jnp.bfloat16)
    self_keys = matmul(rows_self, w_self_k).astype(jnp.bfloat16)
    self_values = matmul(rows_self, w_self_v).astype(jnp.bfloat16)
    self_mixed, self_total = attend_forward(
        self_query, self_keys, self_values, full_lengths, head_size
    )
    d_self_o = gram_left(self_mixed, rows_grad2)
    d_self_mixed = times_transposed(rows_grad2, w_self_o).astype(jnp.bfloat16)
    d_self_query, d_self_keys, d_self_values = attend_backward(
        self_query, self_keys, self_values, d_self_mixed, self_total, full_lengths, head_size
    )
    d_self_q = gram_left(rows_self, d_self_query)
    d_self_k = gram_left(rows_self, d_self_keys)
    d_self_v = gram_left(rows_self, d_self_values)

    def self_term(begin_row, row_count):
        return (
            times_transposed(d_self_query, w_self_q)
            + times_transposed(d_self_keys, w_self_k)
            + times_transposed(d_self_values, w_self_v)
        )

    d_self_rows = back_rows(self_term, own_rows)
    ln_value, ln_pull = jax.vjp(layer_norm, stream1, norm_gain[2], norm_bias[2])
    d_stream1, gain_two, shift_two = ln_pull(d_self_rows)
    grad1 = grad2 + d_stream1
    rows_grad1 = gather_grads(grad1.astype(jnp.bfloat16))
    d_cross_o = gram_left(cross_mixed, rows_grad1)
    d_cross_mixed = times_transposed(rows_grad1, w_cross_o).astype(jnp.bfloat16)
    d_cross_query, d_cross_keys, d_cross_values = attend_backward(
        cross_query, cross_keys, cross_values, d_cross_mixed, cross_total, lengths, head_size
    )
    d_cross_q = gram_left(rows_cross, d_cross_query)
    d_cross_k = gram_left(rows_input, d_cross_keys)
    d_cross_v = gram_left(rows_input, d_cross_values)
    d_lat_rows = back_rows(
        lambda begin_row, row_count: times_transposed(d_cross_query, w_cross_q), own_rows
    )

    def input_term(begin_row, row_count):
        return times_transposed(d_cross_keys, w_cross_k) + times_transposed(
            d_cross_values, w_cross_v
        )

    d_in_rows = back_inputs(input_term, own_inputs)
    ln_value, ln_pull = jax.vjp(layer_norm, stream, norm_gain[0], norm_bias[0])
    d_stream0, gain_zero, shift_zero = ln_pull(d_lat_rows)
    d_latents = grad1 + d_stream0
    ln_value, ln_pull = jax.vjp(layer_norm, source, norm_gain[1], norm_bias[1])
    d_inputs, gain_one, shift_one = ln_pull(d_in_rows)
    gain_grads = jnp.stack([gain_zero, gain_one, gain_two, gain_three])
    shift_grads = jnp.stack([shift_zero, shift_one, shift_two, shift_three])
    bias_grads = jnp.stack([jnp.sum(grad1, axis=0), jnp.sum(grad2, axis=0), jnp.sum(grad3, axis=0)])
    gain_grads, shift_grads, bias_grads = lax.psum(
        (gain_grads, shift_grads, bias_grads), AXES
    )
    (
        d_cross_q,
        d_cross_k,
        d_cross_v,
        d_cross_o,
        d_self_q,
        d_self_k,
        d_self_v,
        d_self_o,
        d_up,
        d_upb,
        d_down,
    ) = (
        lax.psum(d_cross_q.astype(jnp.bfloat16), AXES[0]).astype(jnp.float32),
        lax.psum(d_cross_k.astype(jnp.bfloat16), AXES[0]).astype(jnp.float32),
        lax.psum(d_cross_v.astype(jnp.bfloat16), AXES[0]).astype(jnp.float32),
        lax.psum(d_cross_o.astype(jnp.bfloat16), AXES[0]).astype(jnp.float32),
        lax.psum(d_self_q.astype(jnp.bfloat16), AXES[0]).astype(jnp.float32),
        lax.psum(d_self_k.astype(jnp.bfloat16), AXES[0]).astype(jnp.float32),
        lax.psum(d_self_v.astype(jnp.bfloat16), AXES[0]).astype(jnp.float32),
        lax.psum(d_self_o.astype(jnp.bfloat16), AXES[0]).astype(jnp.float32),
        lax.psum(d_up.astype(jnp.bfloat16), AXES[0]).astype(jnp.float32),
        lax.psum(d_upb.astype(jnp.bfloat16), AXES[0]).astype(jnp.float32),
        lax.psum(d_down.astype(jnp.bfloat16), AXES[0]).astype(jnp.float32),
    )
    return (
        result,
        d_latents,
        d_inputs,
        gain_grads,
        shift_grads,
        bias_grads,
        d_cross_q,
        d_cross_k,
        d_cross_v,
        d_cross_o,
        d_self_q,
        d_self_k,
        d_self_v,
        d_self_o,
        d_up,
        d_upb,
        d_down,
    )


BF = jnp.bfloat16
F32 = jnp.float32
SCALE = HS ** (-0.5)
SELF, KV, QO, DOWN, UP = "self", "kv", "qo", "down", "up"
BIT_X, BIT_CORE, BIT_Y, BIT_Z0, BIT_Z1 = 1, 2, 4, 8, 16
DEVICES = 32
VMEM_LIMIT = 60 << 20


def dg(left, right, left_dim, right_dim):
    return lax.dot_general(
        left, right, (((left_dim,), (right_dim,)), ((), ())), preferred_element_type=F32
    )


def swap(array, bit):
    return lax.ppermute(array, AXES, [(i, i ^ bit) for i in range(DEVICES)])


def total(terms, kind=BF):
    out = terms[0].astype(F32)
    for term in terms[1:]:
        out = out + term.astype(F32)
    return out.astype(kind)


def call(body, name, grid, in_specs, out_specs, out_shape, scalars, operands, scratch=(), aliases=None, flops=0, moved=0):
    spec = pltpu.PrefetchScalarGridSpec(
        num_scalar_prefetch=1, grid=grid, in_specs=in_specs, out_specs=out_specs, scratch_shapes=list(scratch)
    )
    return pl.pallas_call(
        body,
        out_shape=out_shape,
        grid_spec=spec,
        input_output_aliases=aliases or {},
        compiler_params=pltpu.CompilerParams(vmem_limit_bytes=VMEM_LIMIT),
        cost_estimate=pl.CostEstimate(flops=int(flops), bytes_accessed=int(moved), transcendentals=0),
        name=name,
    )(scalars, *operands)


def sds(shape, kind):
    return jax.ShapeDtypeStruct(shape, kind)


def own_quarters(name, groups, scalars, whole):
    operands, specs, outs, shapes, plan = [], [], [], [], []
    for weights, by_rows, part in groups:
        rows, columns = weights[0].shape
        first = len(operands)
        for weight in weights:
            operands.append(weight)
            if by_rows:
                specs.append(pl.BlockSpec((part, columns), lambda i, s: (i ^ s[0], 0)))
            else:
                specs.append(pl.BlockSpec((rows, part), lambda i, s: (0, i ^ s[0])))
        plan.append((first, len(weights), by_rows, part))
        count = 4 if whole else 1
        if by_rows:
            outs.append(pl.BlockSpec((len(weights) * part, columns), lambda i, s: (i, 0)))
            shapes.append(sds((count * len(weights) * part, columns), BF))
        else:
            outs.append(pl.BlockSpec((rows, len(weights) * part), lambda i, s: (0, i)))
            shapes.append(sds((rows, count * len(weights) * part), BF))

    def body(scal_ref, *refs):
        for n, (first, count, by_rows, part) in enumerate(plan):
            out = refs[len(operands) + n]
            for k in range(count):
                cut = slice(k * part, (k + 1) * part)
                if by_rows:
                    out[cut, :] = refs[first + k][...]
                else:
                    out[:, cut] = refs[first + k][...]

    return call(
        body,
        name,
        (4 if whole else 1,),
        specs,
        outs,
        shapes,
        scalars,
        operands,
        moved=sum(shape.size for shape in shapes) * 4,
    )


def enter(name, values, gain, shift, weights, row_block):
    rows, width = values.shape
    count = len(weights)

    def body(scal_ref, v_ref, gain_ref, shift_ref, *refs):
        half = row_block // 2
        for part in range(2):
            cut = slice(part * half, (part + 1) * half)
            v = v_ref[cut, :].astype(F32)
            average = jnp.mean(v, axis=-1, keepdims=True)
            centered = v - average
            scale = lax.rsqrt(jnp.mean(centered * centered, axis=-1, keepdims=True) + EPSILON)
            normed = (centered * scale * gain_ref[...] + shift_ref[...]).astype(BF)
            refs[count][cut, :] = normed
            for k in range(count):
                refs[count + 1 + k][cut, :] = dg(normed, refs[k][...], 1, 0).astype(BF)

    block = pl.BlockSpec((row_block, width), lambda i, s: (i, 0))
    line = pl.BlockSpec((1, width), lambda i, s: (0, 0))
    return call(
        body,
        name,
        (rows // row_block,),
        [block, line, line] + [pl.BlockSpec(w.shape, lambda i, s: (0, 0)) for w in weights],
        [block] + [pl.BlockSpec((row_block, w.shape[1]), lambda i, s: (i, 0)) for w in weights],
        [sds(values.shape, BF)] + [sds((rows, w.shape[1]), BF) for w in weights],
        jnp.zeros((1,), jnp.int32),
        [values, gain, shift, *weights],
        flops=sum(2 * rows * w.size for w in weights),
        moved=rows * width * 8,
    )


def block_of(weight):
    array, rows, columns, row, column = weight
    return pl.BlockSpec((rows, columns), lambda i, s: (row, column))


def project(name, values, weights):
    rows = values.shape[0]
    columns = sum(w[2] for w in weights)

    def body(scal_ref, x_ref, *refs):
        start = 0
        for n, w in enumerate(weights):
            refs[-1][:, start : start + w[2]] = dg(x_ref[...], refs[n][...], 1, 0).astype(BF)
            start += w[2]

    return call(
        body,
        name,
        (1,),
        [pl.BlockSpec(values.shape, lambda i, s: (0, 0))] + [block_of(w) for w in weights],
        pl.BlockSpec((rows, columns), lambda i, s: (0, 0)),
        sds((rows, columns), BF),
        jnp.zeros((1,), jnp.int32),
        [values] + [w[0] for w in weights],
        flops=2 * values.size * columns,
        moved=(values.size + values.shape[1] * columns + rows * columns) * 2,
    )


def mix_norm(name, residual, mixed, weights, bias, gain, shift):
    rows, width = residual.shape
    operands = [residual, bias, gain, shift, *mixed] + [w[0] for w in weights]

    def body(scal_ref, *refs):
        stream_ref, normed_ref, whole = refs[-3:]
        start = 0
        for n, w in enumerate(weights):
            whole[start : start + w[1], :] = refs[4 + len(mixed) + n][...]
            start += w[1]
        branch, start = None, 0
        for n, m in enumerate(mixed):
            term = dg(refs[4 + n][...], whole[start : start + m.shape[1], :], 1, 0)
            branch = term if branch is None else branch + term
            start += m.shape[1]
        for at in range(0, rows, 128):
            cut = slice(at, at + 128)
            out = refs[0][cut, :].astype(F32) + refs[1][...] + branch[cut]
            stream_ref[cut, :] = out
            average = jnp.mean(out, axis=-1, keepdims=True)
            centered = out - average
            scale = lax.rsqrt(jnp.mean(centered * centered, axis=-1, keepdims=True) + EPSILON)
            normed_ref[cut, :] = (centered * scale * refs[2][...] + refs[3][...]).astype(BF)

    block = pl.BlockSpec((rows, width), lambda i, s: (0, 0))
    line = pl.BlockSpec((1, width), lambda i, s: (0, 0))
    total_rows = sum(w[1] for w in weights)
    return call(
        body,
        name,
        (1,),
        [block, line, line, line]
        + [pl.BlockSpec(m.shape, lambda i, s: (0, 0)) for m in mixed]
        + [block_of(w) for w in weights],
        [block, block, pl.BlockSpec((total_rows, width), lambda i, s: (0, 0))],
        [sds((rows, width), F32), sds((rows, width), BF), sds((total_rows, width), BF)],
        jnp.zeros((1,), jnp.int32),
        operands,
        flops=2 * rows * width * total_rows,
        moved=rows * width * 12,
    )


def head(ref, at):
    return ref[:, at * HS : (at + 1) * HS]


def attend(name, arrays, heads_at, lengths, key_rows):
    groups = lengths.shape[0]
    heads = len(heads_at)
    count = len(arrays)

    def body(len_ref, *refs):
        mixed_ref, lse_ref = refs[-2], refs[-1]
        visible = lax.broadcasted_iota(jnp.int32, (key_rows, LAT), 0) < len_ref[pl.program_id(0)]
        width = min(4, heads)
        for first in range(0, heads, width):
            some = heads_at[first : first + width]
            scores = [dg(head(refs[k[0]], k[1]), head(refs[q[0]], q[1]), 1, 1) * SCALE for q, k, v in some]
            scores = [jnp.where(visible, s, NEG_LARGE) for s in scores]
            tops = [jnp.max(s, axis=0, keepdims=True) for s in scores]
            exps = [jnp.exp(s - t) for s, t in zip(scores, tops)]
            sums = [jnp.sum(e, axis=0, keepdims=True) for e in exps]
            probs = [(e * (1.0 / s)).astype(BF) for e, s in zip(exps, sums)]
            for n, (q, k, v) in enumerate(some):
                h = first + n
                mixed_ref[:, h * HS : (h + 1) * HS] = dg(probs[n], head(refs[v[0]], v[1]), 0, 0).astype(BF)
                lse_ref[0, h : h + 1, :] = tops[n] + jnp.log(sums[n])

    return call(
        body,
        name,
        (groups,),
        [pl.BlockSpec((LAT if q else key_rows, a.shape[1]), lambda i, s: (i, 0)) for a, q in arrays],
        [pl.BlockSpec((LAT, heads * HS), lambda i, s: (i, 0)), pl.BlockSpec((1, 8, LAT), lambda i, s: (i, 0, 0))],
        [sds((groups * LAT, heads * HS), BF), sds((groups, 8, LAT), F32)],
        lengths,
        [a for a, _ in arrays],
        flops=groups * heads * key_rows * LAT * HS * 4,
        moved=sum(a.size for a, _ in arrays) * 2,
    )


def attend_back(name, arrays, heads_at, d_mixed, totals, lengths, key_rows, outs, out_at):
    groups = lengths.shape[0]
    operands = [a for a, _ in arrays] + list(d_mixed[0]) + list(totals[0])
    d_base = len(arrays)
    l_base = d_base + len(d_mixed[0])
    count = len(operands)
    heads = len(heads_at)

    def body(len_ref, *refs):
        visible = lax.broadcasted_iota(jnp.int32, (key_rows, LAT), 0) < len_ref[pl.program_id(0)]
        width = min(4, heads)

        def put(spot, value):
            refs[count + spot[0]][:, spot[1] * HS : (spot[1] + 1) * HS] = value.astype(BF)

        for first in range(0, heads, width):
            some = range(first, first + width)
            q = [head(refs[heads_at[h][0][0]], heads_at[h][0][1]) for h in some]
            k = [head(refs[heads_at[h][1][0]], heads_at[h][1][1]) for h in some]
            v = [head(refs[heads_at[h][2][0]], heads_at[h][2][1]) for h in some]
            d = [head(refs[d_base + d_mixed[1][h][0]], d_mixed[1][h][1]) for h in some]
            logs = [refs[l_base + totals[1][h][0]][0, totals[1][h][1] : totals[1][h][1] + 1, :] for h in some]
            scores = [dg(a, b, 1, 1) for a, b in zip(k, q)]
            d_prob = [dg(a, b, 1, 1) for a, b in zip(v, d)]
            probs = [jnp.exp(jnp.where(visible, s * SCALE, NEG_LARGE) - t) for s, t in zip(scores, logs)]
            low_probs = [p.astype(BF) for p in probs]
            inner = [jnp.sum(p * g, axis=0, keepdims=True) for p, g in zip(probs, d_prob)]
            d_score = [(p * (g - i)).astype(BF) for p, g, i in zip(probs, d_prob, inner)]
            for n, h in enumerate(some):
                put(out_at[h][2], dg(low_probs[n], d[n], 1, 0))
                put(out_at[h][1], dg(d_score[n], q[n], 1, 0) * SCALE)
                put(out_at[h][0], dg(d_score[n], k[n], 0, 0) * SCALE)

    return call(
        body,
        name,
        (groups,),
        [pl.BlockSpec((LAT if q else key_rows, a.shape[1]), lambda i, s: (i, 0)) for a, q in arrays]
        + [pl.BlockSpec((LAT, a.shape[1]), lambda i, s: (i, 0)) for a in d_mixed[0]]
        + [pl.BlockSpec((1, 8, LAT), lambda i, s: (i, 0, 0)) for _ in totals[0]],
        [pl.BlockSpec((LAT if q else key_rows, n * HS), lambda i, s: (i, 0)) for q, n in outs],
        [sds((groups * (LAT if q else key_rows), n * HS), BF) for q, n in outs],
        lengths,
        operands,
        flops=groups * heads * key_rows * LAT * HS * 10,
        moved=sum(a.size for a in operands) * 4,
    )


def mlp_block(x, g, up, bias, down):
    cuts = [slice(at, at + 256) for at in range(0, up.shape[1], 256)]
    pre = [dg(x, up[:, c], 1, 0) + bias[:, c] for c in cuts]
    d_hidden = [dg(g, down[c, :], 1, 1) for c in cuts]
    hidden, d_pre, sums = [], [], []
    out = dx = None
    for n, c in enumerate(cuts):
        p = pre[n]
        squared = p * p
        tanh = jnp.tanh(p * (GELU_COEF + (GELU_COEF * GELU_CUBE) * squared))
        half = 0.5 * (1.0 + tanh)
        slope = half + (0.5 * p) * (1.0 - tanh * tanh) * (GELU_COEF + (3.0 * GELU_COEF * GELU_CUBE) * squared)
        hid = (p * half).astype(BF)
        d_wide = d_hidden[n] * slope
        d = d_wide.astype(BF)
        hidden.append(hid)
        d_pre.append(d)
        sums.append(jnp.sum(d_wide, axis=0, keepdims=True))
        term, d_term = dg(hid, down[c, :], 1, 0), dg(d, up[:, c], 1, 1)
        out = term if out is None else out + term
        dx = d_term if dx is None else dx + d_term
    return cuts, hidden, d_pre, sums, out, dx


def mlp_pass(name, normed, grad, up, bias, down, scalars, kind):
    rows, width = normed.shape
    units = up.shape[1] // 4

    def body(scal_ref, x_ref, g_ref, up_ref, b_ref, dn_ref, out_ref, dx_ref, h_ref, p_ref, db_ref, out_sum, dx_sum):
        step = pl.program_id(0)
        cuts, hidden, d_pre, sums, out, dx = mlp_block(x_ref[...], g_ref[...], up_ref, b_ref, dn_ref)
        for n, c in enumerate(cuts):
            h_ref[:, c] = hidden[n]
            p_ref[:, c] = d_pre[n]
            db_ref[:, c] = sums[n]
        out_sum[...] = jnp.where(step == 0, 0.0, out_sum[...]) + out
        dx_sum[...] = jnp.where(step == 0, 0.0, dx_sum[...]) + dx

        @pl.when(step == 3)
        def _():
            out_ref[...] = out_sum[...].astype(kind)
            dx_ref[...] = dx_sum[...].astype(kind)

    fixed = pl.BlockSpec((rows, width), lambda i, s: (0, 0))
    part = pl.BlockSpec((rows, units), lambda i, s: (0, i))
    line = pl.BlockSpec((1, units), lambda i, s: (0, i))
    return call(
        body,
        name,
        (4,),
        [
            fixed,
            fixed,
            pl.BlockSpec((width, units), lambda i, s: (0, i)),
            line,
            pl.BlockSpec((units, width), lambda i, s: (i, 0)),
        ],
        [fixed, fixed, part, part, line],
        [sds((rows, width), kind)] * 2 + [sds((rows, 4 * units), BF)] * 2 + [sds((1, 4 * units), F32)],
        scalars,
        [normed, grad, up, bias, down],
        scratch=[pltpu.VMEM((rows, width), F32)] * 2,
        flops=rows * width * units * 4 * 8,
        moved=4 * rows * width * 4 + up.size * 4,
    )


def z_slot(row, z):
    apart = row ^ z
    return (apart & 1) * 2 + (apart >> 1)


def mlp_grads(name, lefts, rights, scalars):
    rows, width = lefts[0].shape
    units = rights[0].shape[1] // 4
    quarter = width // 4
    count = len(lefts)

    def body(scal_ref, *refs):
        z = scal_ref[1]
        out_ref = refs[-1]
        product = None
        for n in range(count):
            term = dg(refs[n][...], refs[count + n][...], 0, 0)
            product = term if product is None else product + term
        for row in range(4):
            out_ref[0, z_slot(row, z)] = product[row * quarter : (row + 1) * quarter].astype(BF)

    return call(
        body,
        name,
        (2,),
        [pl.BlockSpec((rows, width), lambda i, s: (0, 0))] * count
        + [pl.BlockSpec((rows, units), lambda i, s: (0, i ^ s[0]))] * count,
        pl.BlockSpec((1, 4, quarter, units), lambda i, s: (i, 0, 0, 0)),
        sds((2, 4, quarter, units), BF),
        scalars,
        [*lefts, *rights],
        flops=2 * 2 * rows * width * units * count,
        moved=4 * rows * width * count,
    )


def head_grads(name, pairs, scalars):
    width = pairs[0][0].shape[1]
    quarter = width // 4
    counts = [pair[1].shape[1] // (8 * HS) for pair in pairs]
    weights = sum(counts)

    def body(scal_ref, *refs):
        z = scal_ref[1]
        keep_ref, send_ref = refs[-2], refs[-1]

        def work(out_ref):
            base = 0
            for n, count in enumerate(counts):
                product = dg(refs[2 * n][...], refs[2 * n + 1][...], 0, 0)
                for row in range(4):
                    slot = z_slot(row, z)
                    for near in range(2):
                        for w in range(count):
                            at = (near * count + w) * HS
                            out_ref[0, near, slot, base + w] = product[
                                row * quarter : (row + 1) * quarter, at : at + HS
                            ].astype(BF)
                base += count

        step = pl.program_id(0)

        @pl.when(step < 2)
        def _():
            work(send_ref)

        @pl.when(step >= 2)
        def _():
            work(keep_ref)

    def column(i):
        return (1 - i % 2) * 2 + (1 - i // 2)

    def spot(i):
        return (1 - i % 2, 0, 0, 0, 0, 0)

    specs, operands = [], []
    for (values, grads), count in zip(pairs, counts):
        specs.append(pl.BlockSpec(values.shape, lambda i, s: (0, 0)))
        specs.append(pl.BlockSpec((grads.shape[0], 2 * count * HS), lambda i, s: (0, column(i))))
        operands += [values, grads]
    shape = (2, 2, 4, weights, quarter, HS)
    block = (1, 2, 4, weights, quarter, HS)
    return call(
        body,
        name,
        (4,),
        specs,
        [
            pl.BlockSpec(block, lambda i, s: spot(jnp.maximum(i, 2))),
            pl.BlockSpec(block, lambda i, s: spot(jnp.minimum(i, 1))),
        ],
        [sds(shape, BF)] * 2,
        scalars,
        operands,
        flops=sum(2 * p[0].size * p[1].shape[1] for p in pairs),
        moved=sum(p[0].size + p[1].size for p in pairs) * 2 + 8 * weights * width * HS * 2,
    )


class Sums:
    def __init__(self, own, other):
        self.terms, self.other, self.stage = list(own), other, 0 if other else 1
        self.came = None

    def step(self, line):
        stage = self.stage
        self.stage += 1

        def view(held, at):
            if at is None:
                return held
            for part in at:
                held = held[part]
            return held

        def add(terms, cut):
            return line(
                lambda *held: total([view(h, t[1])[cut] for h, t in zip(held, terms)]), *[t[0] for t in terms]
            )

        if stage > 0 and stage < 4 and self.came is not None:
            self.terms.append((self.came, ()))
        if stage == 0:
            self.came = swap(add(self.other, slice(None)), BIT_X)
        elif stage == 1:
            self.came = swap(add(self.terms, 1), BIT_Y)
            self.terms = [(a, (*at, 0)) for a, at in self.terms]
        elif stage == 2:
            self.came = swap(add(self.terms, slice(2, 4)), BIT_Z0)
            self.terms = [(a, (*at, slice(0, 2))) for a, at in self.terms]
        elif stage == 3:
            self.came = swap(add(self.terms, 1), BIT_Z1)
            self.terms = [(a, (*at, 0)) for a, at in self.terms]
        elif stage == 4:
            self.piece = add(self.terms + [(self.came, ())], slice(None))
            self.came = swap(self.piece, BIT_Z1)
        elif stage == 5:
            self.pair = line(lambda came, piece: jnp.stack([piece, came]), self.came, self.piece)
            self.came = swap(self.pair, BIT_Z0)
        elif stage == 6:
            self.four = line(lambda came, pair: jnp.concatenate([pair, came], axis=0), self.came, self.pair)
            self.near = swap(self.four, BIT_Y)
            self.far = swap(self.four, BIT_CORE)
        elif stage == 7:
            near = line(lambda a: a, self.near)
            self.quarters = [self.four, near, self.far, swap(near, BIT_CORE)]


def finish(name, quarters, turned, scalars, shapes, column, held=()):
    _, weights, quarter, units = quarters[0].shape
    kept = len(held)

    def body(scal_ref, *refs):
        z = scal_ref[1]
        outs = refs[4 + kept :]
        step = pl.program_id(0)
        for k in range(4):

            @pl.when(step == k)
            def _(k=k):
                for row in range(4):
                    slot = z_slot(row, z)
                    for w in range(weights):
                        block = refs[k][slot, w].astype(F32)
                        rows = slice(row * quarter, (row + 1) * quarter)
                        if turned[w]:
                            outs[w][:, rows] = block.T
                        else:
                            outs[w][rows, :] = block

    width = 4 * quarter
    whole = pl.BlockSpec(quarters[0].shape, lambda i, s: (0, 0, 0, 0))
    outs = [
        pl.BlockSpec((units, width), lambda i, s: (column(i ^ s[0]), 0))
        if turned[w]
        else pl.BlockSpec((width, units), lambda i, s: (0, column(i ^ s[0])))
        for w in range(weights)
    ]
    return call(
        body,
        name,
        (4,),
        [whole] * 4 + [pl.BlockSpec(memory_space=pl.ANY)] * kept,
        outs,
        [sds(shape, F32) for shape in shapes],
        scalars,
        [*quarters, *held],
        aliases={1 + 4 + w: w for w in range(kept)},
        moved=weights * width * units * 4 * 6,
    )


def norm_back(name, values, gain, given, products, residual, row_block=512):
    rows, width = values.shape
    operands = [values, gain, *given]
    specs = [
        pl.BlockSpec((row_block, width), lambda i, s: (i, 0)),
        pl.BlockSpec((1, width), lambda i, s: (0, 0)),
    ] + [pl.BlockSpec((row_block, width), lambda i, s: (i, 0))] * len(given)
    spots = []
    for grads, weights in products:
        spots.append((len(operands), [w[2] for w in weights]))
        operands.append(grads)
        specs.append(pl.BlockSpec((row_block, grads.shape[1]), lambda i, s: (i, 0)))
        for weight in weights:
            operands.append(weight[0])
            specs.append(block_of(weight))
    if residual is not None:
        operands.append(residual)
        specs.append(pl.BlockSpec((row_block, width), lambda i, s: (i, 0)))
    count = len(operands)

    def body(scal_ref, *refs):
        outs = refs[count:]
        sums = outs[-1]
        whole = None
        for at, sizes in spots:
            start = 0
            for n, size in enumerate(sizes):
                term = dg(refs[at][:, start : start + size], refs[at + 1 + n][...], 1, 1)
                whole = term if whole is None else whole + term
                start += size
        column_sums = None
        for at in range(0, row_block, 128):
            cut = slice(at, at + 128)
            d = None if whole is None else whole[cut]
            for n in range(len(given)):
                term = refs[2 + n][cut, :].astype(F32)
                d = term if d is None else d + term
            v = refs[0][cut, :].astype(F32)
            average = jnp.mean(v, axis=-1, keepdims=True)
            centered = v - average
            scale = lax.rsqrt(jnp.mean(centered * centered, axis=-1, keepdims=True) + EPSILON)
            unit = centered * scale
            scaled = d * refs[1][...]
            back = scale * (
                scaled
                - jnp.mean(scaled, axis=-1, keepdims=True)
                - unit * jnp.mean(scaled * unit, axis=-1, keepdims=True)
            )
            if residual is not None:
                back = back + refs[count - 1][cut, :].astype(F32)
            outs[0][cut, :] = back
            if residual is not None:
                outs[1][cut, :] = back.astype(BF)
            terms = [jnp.sum(t, axis=0, keepdims=True) for t in (d * unit, d, back)]
            column_sums = terms if column_sums is None else [a + b for a, b in zip(column_sums, terms)]
        first = pl.program_id(0) == 0
        for n in range(3):
            sums[n : n + 1, :] = jnp.where(first, 0.0, sums[n : n + 1, :]) + column_sums[n]

    block = pl.BlockSpec((row_block, width), lambda i, s: (i, 0))
    out_specs = [block] + [block] * (residual is not None) + [pl.BlockSpec((8, width), lambda i, s: (0, 0))]
    out_shape = [sds((rows, width), F32)] + [sds((rows, width), BF)] * (residual is not None) + [sds((8, width), F32)]
    return call(
        body,
        name,
        (rows // row_block,),
        specs,
        out_specs,
        out_shape,
        jnp.zeros((1,), jnp.int32),
        operands,
        flops=sum(2 * g.size * width for g, _ in products),
        moved=rows * width * 12,
    )


def row_shards(
    latents,
    inputs,
    frames,
    group_clip,
    norm_gain,
    norm_bias,
    cross_q,
    cross_k,
    cross_v,
    cross_o,
    self_q,
    self_k,
    self_v,
    self_o,
    mlp_up,
    up_bias,
    mlp_down,
    out_bias,
    cotangent,
):
    dp = lax.axis_index(AXES[0])
    core, near, z = dp & 1, (dp >> 1) & 1, dp >> 2
    mine = 2 * core + near
    scalars = jnp.stack([mine, z]).astype(jnp.int32)
    own_groups = latents.shape[0] // LAT
    key_rows = inputs.shape[0] // own_groups

    width = latents.shape[1]
    units = mlp_up.shape[1] // 4
    last = [scalars]

    def line(work, *args):
        first, _ = lax.optimization_barrier((args[0], last[0]))
        out = work(first, *args[1:])
        last[0] = jax.tree.leaves(out)[0]
        return out

    def low_matmul(left, right):
        return matmul(left, right).astype(BF)

    def low_turned(left, right):
        return times_transposed(left, right).astype(BF)

    def settle(array):
        last[0], out = lax.optimization_barrier((last[0], array))
        return out

    class Fetch:
        def __init__(self, piece):
            self.quarters = [swap(piece, BIT_X), None, None, None]

        def near(self):
            q = self.quarters
            q[0] = settle(q[0])
            q[1], q[2] = swap(q[0], BIT_Y), swap(q[0], BIT_CORE)

        def far(self):
            q = self.quarters
            q[1] = settle(q[1])
            q[3] = swap(q[1], BIT_CORE)

    matches = group_clip[:, None] == lax.broadcasted_iota(jnp.int32, (1, frames.shape[0]), 1)
    lengths = jnp.sum(jnp.where(matches, frames[None, :], 0), axis=1) * FRAME_ROWS
    lengths = lax.dynamic_slice_in_dim(lengths, lax.axis_index(AXES[1]) * own_groups, own_groups, 0)
    lengths = lengths.astype(jnp.int32)
    full = jnp.full((own_groups,), LAT, jnp.int32)
    gains = [norm_gain[n : n + 1] for n in range(4)]
    shifts = [norm_bias[n : n + 1] for n in range(4)]

    kv_near, q_near, o_near, s_near = line(
        lambda s: own_quarters(
            "pieces",
            [
                ([cross_k, cross_v], False, HS),
                ([cross_q], False, HS),
                ([cross_o, self_o], True, HS),
                ([self_q, self_k, self_v], False, HS),
            ],
            s,
            False,
        ),
        scalars,
    )
    kv, q, o, s3 = Fetch(kv_near), Fetch(q_near), Fetch(o_near), Fetch(s_near)
    own_bias = up_bias.astype(F32)[None]
    low3 = cotangent
    low3_core = swap(low3, BIT_CORE)

    (kv_own,) = line(lambda s: own_quarters("own_kv", [([cross_k, cross_v], False, HS)], s, True), scalars)
    in_normed, keyval_own = line(
        lambda x: enter("enter_inputs", x, gains[1], shifts[1], [kv_own], 512), inputs
    )
    kv.near()
    low3_x = swap(low3, BIT_X)
    q_own, o_own, s_own = line(
        lambda s: own_quarters(
            "own_rest",
            [([cross_q], False, HS), ([cross_o, self_o], True, HS), ([self_q, self_k, self_v], False, HS)],
            s,
            True,
        ),
        scalars,
    )
    q.near()
    lat_normed, query_own = line(lambda x: enter("enter_latents", x, gains[0], shifts[0], [q_own], 512), latents)
    kv.far()
    mixed_own, total_own = line(
        lambda q: attend(
            "cross_own",
            [(q, True), (keyval_own, False)],
            [((0, j), (1, 2 * j), (1, 2 * j + 1)) for j in range(4)],
            lengths,
            key_rows,
        ),
        query_own,
    )
    q.far()
    o.near()
    keyval_other = [None] * 4
    for j in (0, 2, 1, 3):
        keyval_other[j] = line(lambda w: low_matmul(in_normed, w), kv.quarters[j])
    o.far()
    query_other = line(
        lambda x: project("query_other", x, [(w, width, HS, 0, 0) for w in q.quarters]), lat_normed
    )
    mixed_other, total_other = line(
        lambda q: attend(
            "cross_other",
            [(q, True)] + [(a, False) for a in keyval_other],
            [((0, j), (1 + j, 0), (1 + j, 1)) for j in range(4)],
            lengths,
            key_rows,
        ),
        query_other,
    )
    s3.near()
    stream1, self_normed, co = line(
        lambda m: mix_norm(
            "mix_norm1",
            latents,
            [m, mixed_other],
            [(o_own, HS, width, 2 * j, 0) for j in range(4)] + [(w, HS, width, 0, 0) for w in o.quarters],
            out_bias[0:1],
            gains[2],
            shifts[2],
        ),
        mixed_own,
    )
    s3.far()
    qkv = line(
        lambda x: project(
            "qkv", x, [(s_own, width, 12 * HS, 0, 0)] + [(w, width, 3 * HS, 0, 0) for w in s3.quarters]
        ),
        self_normed,
    )
    self_heads = [((0, 3 * j), (0, 3 * j + 1), (0, 3 * j + 2)) for j in range(8)]
    smix, stotal = line(lambda q: attend("self", [(q, True)], self_heads, full, LAT), qkv)
    stream2, mlp_normed, so = line(
        lambda m: mix_norm(
            "mix_norm2",
            stream1,
            [m],
            [(o_own, HS, width, 2 * j + 1, 0) for j in range(4)] + [(w, HS, width, 1, 0) for w in o.quarters],
            out_bias[1:2],
            gains[3],
            shifts[3],
        ),
        smix,
    )

    mlp_x, mlp_core = swap(mlp_normed, BIT_X), swap(mlp_normed, BIT_CORE)
    low3_x = settle(low3_x)
    low3_x_core = swap(low3_x, BIT_CORE)
    out_own, dx_own, h_own, p_own, db_own = line(
        lambda x: mlp_pass("mlp_own", x, low3, mlp_up, own_bias, mlp_down, scalars, F32), mlp_normed
    )
    h_core, p_core = swap(h_own, BIT_CORE), swap(p_own, BIT_CORE)
    out_send, dx_send, h_x, p_x, db_x = line(
        lambda x: mlp_pass("mlp_x", x, low3_x, mlp_up, own_bias, mlp_down, scalars, BF), mlp_x
    )
    dx_came = swap(dx_send, BIT_X)
    h_x_core, p_x_core = swap(h_x, BIT_CORE), swap(p_x, BIT_CORE)
    mlp_x_core = swap(mlp_x, BIT_CORE)
    out_came = swap(out_send, BIT_X)

    v, pieces, done = SimpleNamespace(), {}, {}

    def norm_back3():
        v.grad2, v.low2, v.sums3 = line(
            lambda d: norm_back("norm_back3", stream2, gains[3], [d, dx_came], [], cotangent), dx_own
        )

    def down_grads():
        piece = line(
            lambda g: mlp_grads(
                "down_grads", [g, low3_x, low3_core, low3_x_core], [h_own, h_x, h_core, h_x_core], scalars
            ),
            low3,
        )
        pieces[DOWN] = Sums([(piece, ())], [])

    def up_grads():
        piece = line(
            lambda x: mlp_grads("up_grads", [x, mlp_x, mlp_core, mlp_x_core], [p_own, p_x, p_core, p_x_core], scalars),
            mlp_normed,
        )
        pieces[UP] = Sums([(piece, ())], [])

    def self_back():
        d_smix = line(low_turned, v.low2, so)
        (v.d_qkv,) = line(
            lambda q: attend_back(
                "self_back",
                [(q, True)],
                self_heads,
                ((d_smix,), [(0, j) for j in range(8)]),
                ((stotal,), [(0, j) for j in range(8)]),
                full,
                LAT,
                [(True, 24)],
                self_heads,
            ),
            qkv,
        )

    def self_grads():
        keep, send = line(
            lambda x: head_grads("self_grads", [(x, v.d_qkv), (v.low2, smix)], scalars), self_normed
        )
        came = swap(send, BIT_CORE)
        pieces[SELF] = Sums([(keep, (0,)), (came, (0,))], [(keep, (1,)), (came, (1,))])

    def norm_back2():
        v.grad1, v.low1, v.sums2 = line(
            lambda d: norm_back("norm_back2", stream1, gains[2], [], [(d, [(s_own, width, 12 * HS, 0, 0)] + [(w, width, 3 * HS, 0, 0) for w in s3.quarters])], v.grad2),
            v.d_qkv,
        )

    def cross_back():
        d_mix = line(low_turned, v.low1, co)
        v.d_query, v.d_keyval = line(
            lambda q: attend_back(
                "cross_back",
                [(q, True), (query_other, True), (keyval_own, False)] + [(a, False) for a in keyval_other],
                [((0, j), (2, 2 * j), (2, 2 * j + 1)) for j in range(4)]
                + [((1, j), (3 + j, 0), (3 + j, 1)) for j in range(4)],
                ((d_mix,), [(0, j) for j in range(8)]),
                ((total_own, total_other), [(j // 4, j % 4) for j in range(8)]),
                lengths,
                key_rows,
                [(True, 8), (False, 16)],
                [((0, j), (1, 2 * j), (1, 2 * j + 1)) for j in range(8)],
            ),
            query_own,
        )

    def kv_grads():
        keep, send = line(lambda x: head_grads("kv_grads", [(x, v.d_keyval)], scalars), in_normed)
        came = swap(send, BIT_CORE)
        pieces[KV] = Sums([(keep, (0,)), (came, (0,))], [(keep, (1,)), (came, (1,))])

    def q_grads():
        mix = line(lambda a, b: jnp.concatenate([a, b], axis=1), mixed_own, mixed_other)
        keep, send = line(
            lambda x: head_grads("q_grads", [(x, v.d_query), (v.low1, mix)], scalars), lat_normed
        )
        came = swap(send, BIT_CORE)
        pieces[QO] = Sums([(keep, (0,)), (came, (0,))], [(keep, (1,)), (came, (1,))])

    def norm_back1():
        v.d_inputs, v.sums1 = line(
            lambda d: norm_back("norm_back1", inputs, gains[1], [], [(d, [(kv_own, width, 8 * HS, 0, 0)] + [(w, width, 2 * HS, 0, 0) for w in kv.quarters])], None),
            v.d_keyval,
        )

    def norm_back0():
        v.d_latents, _, v.sums0 = line(
            lambda d: norm_back("norm_back0", latents, gains[0], [], [(d, [(q_own, width, 4 * HS, 0, 0)] + [(w, width, HS, 0, 0) for w in q.quarters])], v.grad1),
            v.d_query,
        )

    def result():
        v.result = line(
            lambda a: (stream2 + (a + out_came.astype(F32)) + out_bias[2]).astype(BF),
            out_own,
        )

    def small():
        every = [v.sums0, v.sums1, v.sums2, v.sums3]
        shared = [a[0] for a in every] + [a[1] for a in every]
        shared += [v.sums2[2], v.sums3[2], jnp.sum(cotangent.astype(F32), axis=0)]
        v.small = line(lambda a, *rest: jnp.stack([a, *rest]), *shared)

    def small_x():
        units_sums = (db_own + db_x).reshape(-1, width)
        v.small = line(
            lambda a, b, c: jnp.concatenate([a + b, c], axis=0), v.small, swap(v.small, BIT_X), units_sums
        )

    def small_step(bit):
        def run():
            v.small = line(lambda a, b: a + b, v.small, swap(v.small, bit))

        return run

    def finish_heads(key, turned, shapes):
        def run():
            done[key] = line(
                lambda f: finish(
                    key + "_finish", [f, *pieces[key].quarters[1:]], turned, scalars, shapes, lambda q: q
                ),
                pieces[key].quarters[0],
            )

        return run

    def finish_mlp(key, turned, shape):
        def run():
            done[key] = line(
                lambda f: finish(
                    key + "_finish",
                    [q[:, None] for q in [f, *pieces[key].quarters[1:]]],
                    [turned],
                    scalars,
                    [shape],
                    lambda q: q,
                ),
                pieces[key].quarters[0],
            )

        return run

    order = (
        down_grads,
        up_grads,
        DOWN,
        norm_back3,
        self_back,
        self_grads,
        UP,
        norm_back2,
        SELF,
        DOWN,
        cross_back,
        DOWN,
        UP,
        kv_grads,
        DOWN,
        UP,
        KV,
        q_grads,
        DOWN,
        UP,
        QO,
        SELF,
        DOWN,
        UP,
        norm_back1,
        UP,
        SELF,
        DOWN,
        norm_back0,
        small,
        UP,
        SELF,
        KV,
        result,
        small_x,
        SELF,
        KV,
        QO,
        small_step(BIT_CORE),
        finish_mlp(DOWN, True, mlp_down.shape),
        SELF,
        KV,
        QO,
        small_step(BIT_Y),
        finish_mlp(UP, False, mlp_up.shape),
        SELF,
        KV,
        QO,
        small_step(BIT_Z0),
        KV,
        QO,
        small_step(BIT_Z1),
        SELF,
        KV,
        QO,
        finish_heads(SELF, [False] * 3 + [True], [cross_q.shape] * 3 + [cross_o.shape]),
        KV,
        QO,
        finish_heads(KV, [False] * 2, [cross_q.shape] * 2),
        QO,
        finish_heads(QO, [False, True], [cross_q.shape, cross_o.shape]),
    )
    for work in order:
        if isinstance(work, str):
            pieces[work].step(line)
        else:
            work()
    d_self_q, d_self_k, d_self_v, d_self_o = done[SELF]
    d_cross_k, d_cross_v = done[KV]
    d_cross_q, d_cross_o = done[QO]
    sums = v.small
    return (
        v.result,
        v.d_latents,
        v.d_inputs,
        sums[0:4],
        sums[4:8],
        sums[8:11],
        d_cross_q,
        d_cross_k,
        d_cross_v,
        d_cross_o,
        d_self_q,
        d_self_k,
        d_self_v,
        d_self_o,
        done[UP][0],
        sums[11:].reshape(-1),
        done[DOWN][0],
    )


def solution(mesh):
    rows, columns, heads, whole = P(AXES, None), P(None, AXES[1]), P(AXES[1], None), P()
    in_specs = (
        rows, rows, whole, P(AXES[0]), whole, whole, columns, columns, columns, heads, columns, columns, columns, heads,
        columns, P(AXES[1]), heads, whole, rows,
    )
    out_specs = (
        rows, rows, rows, whole, whole, whole, columns, columns, columns, heads, columns, columns, columns, heads,
        columns, P(AXES[1]), heads,
    )
    paired = mesh.shape[AXES[0]] == 16 and mesh.shape[AXES[1]] == 2
    shards = row_shards if paired else split_shards
    return jax.shard_map(shards, mesh=mesh, in_specs=in_specs, out_specs=out_specs, check_vma=False)
```
